32 devices in a mesh: rows: 4 (over z), cols: 8 (over y, x, core).
Axes of the slice: x: 2, y: 2, z: 4, core: 2. Of those that a mesh axis runs over, the one named last changes fastest.
Arguments:
- imagery: bfloat16 [64, 128, 192], P('rows', 'cols'), may hold values from -6 to 6
- cotangent: bfloat16 [64, 128, 192], P('rows', 'cols'), may hold values from -6 to 6
- norm_gain: float32 [2, 192], replicated, may hold values from 0.5 to 1.5
- norm_bias: float32 [2, 192], replicated, may hold values from -3 to 3
- qkv_weight: bfloat16 [2, 192, 576], replicated, may hold values from -0.4375 to 0.4375
- qkv_bias: float32 [2, 576], replicated, may hold values from -3 to 3
- rel_table: float32 [2, 6, 225], replicated, may hold values from -4 to 330
- proj_weight: bfloat16 [2, 192, 192], replicated, may hold values from -0.4375 to 0.4375
- proj_bias: float32 [2, 192], replicated, may hold values from -3 to 3
- mlp_gain: float32 [2, 192], replicated, may hold values from 0.5 to 1.5
- mlp_bias: float32 [2, 192], replicated, may hold values from -3 to 3
- up_weight: bfloat16 [2, 192, 768], replicated, may hold values from -0.4375 to 0.4375
- up_bias: float32 [2, 768], replicated, may hold values from -3 to 3
- down_weight: bfloat16 [2, 768, 192], replicated, may hold values from -0.21875 to 0.21875
- down_bias: float32 [2, 192], replicated, may hold values from -3 to 3
Outputs:
- output: bfloat16 [64, 128, 192], P('rows', 'cols')
- imagery_grad: bfloat16 [64, 128, 192], P('rows', 'cols')
- norm_gain_grad: float32 [2, 192], replicated
- norm_bias_grad: float32 [2, 192], replicated
- qkv_weight_grad: float32 [2, 192, 576], replicated
- qkv_bias_grad: float32 [2, 576], replicated
- rel_table_grad: float32 [2, 6, 225], replicated
- proj_weight_grad: float32 [2, 192, 192], replicated
- proj_bias_grad: float32 [2, 192], replicated
- mlp_gain_grad: float32 [2, 192], replicated
- mlp_bias_grad: float32 [2, 192], replicated
- up_weight_grad: float32 [2, 192, 768], replicated
- up_bias_grad: float32 [2, 768], replicated
- down_weight_grad: float32 [2, 768, 192], replicated
- down_bias_grad: float32 [2, 192], replicated
The draws below stay inside these ranges and needn't reach their ends.
All inputs are finite; a program needn't handle non-finite values.
Results may differ from the reference program's by a relative error of at most 0.02.
Values may be sent and summed in bfloat16 or wider, within the bound.
A program may use at most 128 MiB of HBM per device.

```python
import jax
import jax.numpy as jnp
import numpy as np
from jax import lax

C = 192
HEADS = 6
MLP = 768
WIN = 8
TILE = 16
HEIGHT = 64
WIDTH = 128
N_ROWS = 4
N_COLS = 8


def draw_rel_table(key, part):
    columns = (2 * WIN - 1) ** 2
    return jnp.clip(jax.random.normal(key, (2, HEADS, columns), jnp.float32), -4.0, 4.0)


def levels(key, shape, pieces, low, high):
    loudness = 1.0
    for dim, parts in pieces:
        draws = jax.random.uniform(jax.random.fold_in(jax.random.fold_in(key, 6), dim), (parts,), jnp.float32, low / len(pieces), high / len(pieces))
        loudness = loudness * jnp.repeat(jnp.exp(draws), shape[dim] // parts).reshape((-1,) + (1,) * (len(shape) - 1 - dim))
    return loudness


def normal_values(own_key, extent, deviation, most, shards=(), kind=jnp.bfloat16):
    entries = jax.random.normal(own_key, extent, jnp.float32) * deviation
    if len(shards) > 0:
        entries = levels(own_key, extent, shards, -0.22, 0.18) * entries
    return jnp.clip(entries, min=-most, max=most).astype(kind)


def setup_inputs(seed: int = 0) -> dict:
    streams_of = jax.random.split(jax.random.key(seed), 16)
    imagery = normal_values(streams_of[0], (HEIGHT, WIDTH, C), 1.0, 6.0, ((0, 4), (1, 8)))
    cotangent = normal_values(streams_of[1], (HEIGHT, WIDTH, C), 1.0, 6.0, ((0, 4), (1, 8)))
    norm_gain = jnp.clip(1.0 + 0.1 * jax.random.normal(streams_of[2], (2, C), jnp.float32), 0.5, 1.5)
    norm_bias = normal_values(streams_of[3], (2, C), 0.5, 3.0, (), jnp.float32)
    qkv_weight = normal_values(streams_of[4], (2, C, 3 * C), C ** -0.5, 0.4375)
    qkv_bias = normal_values(streams_of[5], (2, 3 * C), 0.5, 3.0, (), jnp.float32)
    rel_table = draw_rel_table(jax.random.fold_in(streams_of[15], 71), 0)
    proj_weight = normal_values(streams_of[7], (2, C, C), C ** -0.5, 0.4375)
    proj_bias = normal_values(streams_of[8], (2, C), 0.5, 3.0, (), jnp.float32)
    mlp_gain = jnp.clip(1.0 + 0.1 * jax.random.normal(streams_of[9], (2, C), jnp.float32), 0.5, 1.5)
    mlp_bias = normal_values(streams_of[10], (2, C), 0.5, 3.0, (), jnp.float32)
    up_weight = normal_values(streams_of[11], (2, C, MLP), C ** -0.5, 0.4375)
    up_bias = normal_values(streams_of[12], (2, MLP), 0.5, 3.0, (), jnp.float32)
    down_weight = normal_values(streams_of[13], (2, MLP, C), MLP ** -0.5, 0.21875)
    down_bias = normal_values(streams_of[14], (2, C), 0.5, 3.0, (), jnp.float32)
    return dict(imagery=imagery, cotangent=cotangent, norm_gain=norm_gain, norm_bias=norm_bias, qkv_weight=qkv_weight, qkv_bias=qkv_bias, rel_table=rel_table, proj_weight=proj_weight, proj_bias=proj_bias, mlp_gain=mlp_gain, mlp_bias=mlp_bias, up_weight=up_weight, up_bias=up_bias, down_weight=down_weight, down_bias=down_bias)


EPSILON = 1e-05

def norm_rows(values, norm_scale, norm_shift):
    widened = values.astype(jnp.float32)
    center = widened - lax.optimization_barrier(jnp.mean(widened, axis=-1, keepdims=True))
    spread = lax.optimization_barrier(jnp.mean(center * center, axis=-1, keepdims=True))
    return (center * lax.rsqrt(spread + EPSILON) * norm_scale + norm_shift).astype(jnp.bfloat16)

def offset_table(window):
    cells = np.arange(window * window)
    row_of = cells // window
    col_of = cells % window
    offsets = (row_of[:, None] - row_of[None, :] + window - 1) * (2 * window - 1) + (col_of[:, None] - col_of[None, :] + window - 1)
    return (offsets.reshape(-1)[:, None] == np.arange((2 * window - 1) ** 2)[None, :]).astype(np.float32)

def to_windows(values, window):
    height, breadth, features = values.shape
    blocked = values.reshape(height // window, window, breadth // window, window, features)
    return blocked.transpose(0, 2, 1, 3, 4).reshape(-1, window * window, features)

def from_windows(values, height, breadth, window):
    features = values.shape[-1]
    blocked = values.reshape(height // window, breadth // window, window, window, features)
    return blocked.transpose(0, 2, 1, 3, 4).reshape(height, breadth, features)

def swin_block(inputs, params, row_start, col_start, total_rows, total_cols, masked):
    norm_gain, norm_bias, qkv_weight, qkv_bias, rel_table, proj_weight, proj_bias, mlp_gain, mlp_bias, up_weight, up_bias, down_weight, down_bias = params
    height, breadth, channels = inputs.shape
    head_count = rel_table.shape[0]
    head_size = channels // head_count
    window = WIN
    normed = norm_rows(inputs, norm_gain, norm_bias).reshape(height * breadth, channels)
    packed = (jnp.dot(normed, qkv_weight, preferred_element_type=jnp.float32) + qkv_bias).astype(jnp.bfloat16)
    grouped = to_windows(packed.reshape(height, breadth, 3 * channels), window)
    grouped = grouped.reshape(grouped.shape[0], window * window, 3, head_count, head_size)
    queries = grouped[:, :, 0]
    keys_win = grouped[:, :, 1]
    values_win = grouped[:, :, 2]
    scores = jnp.einsum('nqhd,nkhd->nhqk', queries, keys_win, preferred_element_type=jnp.float32) * head_size ** (-0.5)
    position = jnp.dot(rel_table, jnp.asarray(offset_table(window)).T, precision=lax.Precision.HIGHEST)
    scores = scores + position.reshape(head_count, window * window, window * window)[None]
    if masked:
        row_ids = row_start + jnp.arange(height, dtype=jnp.int32)
        col_ids = col_start + jnp.arange(breadth, dtype=jnp.int32)
        row_zone = (row_ids >= total_rows - window).astype(jnp.int32) + (row_ids >= total_rows - window // 2).astype(jnp.int32)
        col_zone = (col_ids >= total_cols - window).astype(jnp.int32) + (col_ids >= total_cols - window // 2).astype(jnp.int32)
        zones = (row_zone[:, None] * 3 + col_zone[None, :])[:, :, None]
        zones = to_windows(zones, window)[:, :, 0]
        same_zone = zones[:, :, None] == zones[:, None, :]
        scores = jnp.where(same_zone[:, None], scores, -1e+30)
    row_max = lax.stop_gradient(lax.optimization_barrier(jnp.max(scores, axis=-1, keepdims=True)))
    powers = jnp.exp(scores - row_max)
    attention = (powers / lax.optimization_barrier(jnp.sum(powers, axis=-1, keepdims=True))).astype(jnp.bfloat16)
    mixed_out = jnp.einsum('nhqk,nkhd->nqhd', attention, values_win, preferred_element_type=jnp.float32).astype(jnp.bfloat16)
    mixed_out = from_windows(mixed_out.reshape(mixed_out.shape[0], window * window, channels), height, breadth, window)
    attended = jnp.dot(mixed_out.reshape(height * breadth, channels), proj_weight, preferred_element_type=jnp.float32) + proj_bias
    middle = (inputs.astype(jnp.float32) + attended.reshape(height, breadth, channels)).astype(jnp.bfloat16)
    normed_mid = norm_rows(middle, mlp_gain, mlp_bias).reshape(height * breadth, channels)
    hidden = jax.nn.gelu(jnp.dot(normed_mid, up_weight, preferred_element_type=jnp.float32) + up_bias, approximate=False).astype(jnp.bfloat16)
    output = middle.astype(jnp.float32) + (jnp.dot(hidden, down_weight, preferred_element_type=jnp.float32) + down_bias).reshape(height, breadth, channels)
    return output.astype(jnp.bfloat16)

def reference(imagery, cotangent, norm_gain, norm_bias, qkv_weight, qkv_bias, rel_table, proj_weight, proj_bias, mlp_gain, mlp_bias, up_weight, up_bias, down_weight, down_bias):
    params = (norm_gain, norm_bias, qkv_weight, qkv_bias, rel_table, proj_weight, proj_bias, mlp_gain, mlp_bias, up_weight, up_bias, down_weight, down_bias)
    first = tuple((member[0] for member in params))
    second = tuple((member[1] for member in params))
    height = TILE * N_ROWS
    breadth = TILE * N_COLS
    tile_count = N_ROWS * N_COLS
    half_window = WIN // 2

    def to_tiles(values):
        return values.reshape(N_ROWS, TILE, N_COLS, TILE, C).transpose(0, 2, 1, 3, 4).reshape(tile_count, TILE, TILE, C)

    def from_tiles(values):
        return values.reshape(N_ROWS, N_COLS, TILE, TILE, C).transpose(0, 2, 1, 3, 4).reshape(height, breadth, C)
    row_starts = jnp.arange(tile_count, dtype=jnp.int32) // N_COLS * TILE
    col_starts = jnp.arange(tile_count, dtype=jnp.int32) % N_COLS * TILE
    image_tiles = to_tiles(imagery)
    level_one = from_tiles(lax.map(lambda member: swin_block(member, first, 0, 0, height, breadth, False), image_tiles))
    moved = to_tiles(jnp.roll(level_one, (-half_window, -half_window), (0, 1)))
    moved_back = to_tiles(jnp.roll(cotangent, (-half_window, -half_window), (0, 1)))

    def second_step(totals, items):
        inputs, grad_in, row_at, col_at = items

        def local(values, weights):
            return swin_block(values, weights, row_at, col_at, height, breadth, True)
        result, pull = jax.vjp(local, inputs, second)
        grad_values, grad_weights = pull(grad_in)
        totals = tuple((total + member.astype(jnp.float32) for total, member in zip(totals, grad_weights)))
        return (totals, (result, grad_values))
    zero_two = tuple((jnp.zeros(member.shape, jnp.float32) for member in second))
    grads_two, (level_two, back_two) = lax.scan(second_step, zero_two, (moved, moved_back, row_starts, col_starts))
    output = jnp.roll(from_tiles(level_two), (half_window, half_window), (0, 1))
    back_in = to_tiles(jnp.roll(from_tiles(back_two), (half_window, half_window), (0, 1)))

    def first_step(totals, items):
        inputs, grad_in = items

        def local(values, weights):
            return swin_block(values, weights, 0, 0, height, breadth, False)
        result, pull = jax.vjp(local, inputs, first)
        grad_values, grad_weights = pull(grad_in)
        totals = tuple((total + member.astype(jnp.float32) for total, member in zip(totals, grad_weights)))
        return (totals, grad_values)
    zero_one = tuple((jnp.zeros(member.shape, jnp.float32) for member in first))
    grads_one, back_one = lax.scan(first_step, zero_one, (image_tiles, back_in))
    imagery_grad = from_tiles(back_one)
    factor = float(height * breadth) ** (-0.5)
    grads = [jnp.stack([lower, upper]) * factor for lower, upper in zip(grads_one, grads_two)]
    return (output, imagery_grad, grads[0], grads[1], grads[2], grads[3], grads[4], grads[5], grads[6], grads[7], grads[8], grads[9], grads[10], grads[11], grads[12])
```

```python
import functools

import jax
import jax.numpy as jnp
from jax import lax
from jax.experimental import pallas as pl
from jax.experimental.pallas import tpu as pltpu
from jax.sharding import PartitionSpec as P

WIN = 8
EPSILON = 1e-05
F32 = jnp.float32
BF16 = jnp.bfloat16
MESH = pl.DeviceIdType.MESH


def mm(a, b):
    return jnp.dot(a, b, preferred_element_type=F32)


def mm_nt(a, b):
    return lax.dot_general(a, b, (((1,), (1,)), ((), ())), preferred_element_type=F32)


def mm_tn(a, b):
    return lax.dot_general(a, b, (((0,), (0,)), ((), ())), preferred_element_type=F32)


def split3(x):
    hi = x.astype(BF16)
    rest = x - hi.astype(F32)
    mid = rest.astype(BF16)
    return hi, mid, (rest - mid.astype(F32)).astype(BF16)


def load_windows(ref, height, breadth):
    parts = []
    for r in range(0, height, WIN):
        for c in range(0, breadth, WIN):
            piece = ref[r : r + WIN, c : c + WIN, :].astype(F32)
            parts.append(piece.reshape(WIN * WIN, piece.shape[-1]))
    return jnp.concatenate(parts, axis=0)


def store_windows(ref, values, height, breadth):
    at = 0
    for r in range(0, height, WIN):
        for c in range(0, breadth, WIN):
            piece = values[at : at + WIN * WIN].reshape(WIN, WIN, values.shape[-1])
            ref[r : r + WIN, c : c + WIN, :] = piece.astype(ref.dtype)
            at += WIN * WIN


def norm_parts(x):
    center = x - jnp.mean(x, axis=-1, keepdims=True)
    spread = jnp.mean(center * center, axis=-1, keepdims=True)
    inv = lax.rsqrt(spread + EPSILON)
    return center * inv, inv


def norm_back(unit, inv, gain, grad):
    scaled = grad * gain
    m1 = jnp.mean(scaled, axis=-1, keepdims=True)
    m2 = jnp.mean(scaled * unit, axis=-1, keepdims=True)
    return inv * (scaled - m1 - unit * m2)


def rnd(x):
    return x.astype(BF16).astype(F32)


def head_rows(rows, heads, size):
    lane = lax.broadcasted_iota(jnp.int32, (heads * rows, heads * size), 1)
    row = lax.broadcasted_iota(jnp.int32, (heads * rows, heads * size), 0)
    return (lane // size) == (row // rows)


def spread_heads(x, mask, heads):
    tiled = jnp.concatenate([x] * heads, axis=0)
    return jnp.where(mask, tiled, jnp.zeros_like(tiled))


def fold_heads(x, mask, heads, rows):
    kept = jnp.where(mask, x, 0.0)
    total = kept[:rows]
    for h in range(1, heads):
        total = total + kept[h * rows : (h + 1) * rows]
    return total


def cell_code(n, dim, shape):
    index = lax.broadcasted_iota(jnp.int32, shape, dim)
    return (index // WIN) * (2 * WIN - 1) + index % WIN


def position_stack(rel, heads):
    cells = WIN * WIN
    span = 2 * WIN - 1
    middle = (span * span - 1) // 2
    width = 256
    lanes = lax.broadcasted_iota(jnp.int32, (cells, 128), 1)
    pick = (lanes == cell_code(cells, 0, (cells, 128))).astype(BF16)
    outs = []
    for h in range(heads):
        row = jnp.concatenate([rel[h : h + 1], jnp.zeros((1, width - span * span), F32)], axis=1)
        row = jnp.broadcast_to(row, (WIN, width))
        rolled = [
            pltpu.roll(row, (span * y - middle) % width, 1, stride=1, stride_axis=0)[:, :128]
            for y in range(WIN)
        ]
        parts = split3(jnp.concatenate(rolled, axis=0))
        outs.append(mm_nt(pick, parts[0]) + mm_nt(pick, parts[1]) + mm_nt(pick, parts[2]))
    return jnp.concatenate(outs, axis=0)


def position_grad(dstack, heads):
    cells = WIN * WIN
    span = 2 * WIN - 1
    middle = (span * span - 1) // 2
    width = 256
    lanes = lax.broadcasted_iota(jnp.int32, (cells, width), 1)
    pick = (lanes == middle - cell_code(cells, 0, (cells, width))).astype(BF16)
    rows = []
    for h in range(heads):
        hi, mid, _ = split3(dstack[h * cells : (h + 1) * cells])
        flipped = mm_tn(hi, pick) + mm_tn(mid, pick)
        total = None
        for y in range(WIN):
            part = pltpu.roll(
                flipped[y * WIN : (y + 1) * WIN], span * y, 1, stride=1, stride_axis=0
            )
            total = part if total is None else total + part
        rows.append(jnp.sum(total, axis=0, keepdims=True))
    rows.append(jnp.zeros((16 - heads, width), F32))
    stacked = jnp.concatenate(rows, axis=0)
    back = (
        lax.broadcasted_iota(jnp.int32, (width, width), 0)
        + lax.broadcasted_iota(jnp.int32, (width, width), 1)
        == span * span - 1
    ).astype(BF16)
    hi, mid, _ = split3(stacked)
    return mm(hi, back) + mm(mid, back)


def zone_masks(start_ref, height, breadth, total_rows, total_cols, heads):
    cells = WIN * WIN
    masks = []
    for r in range(0, height, WIN):
        for c in range(0, breadth, WIN):

            def zone(dim):
                index = lax.broadcasted_iota(jnp.int32, (heads * cells, cells), dim) % cells
                row = start_ref[0] + r + index // WIN
                col = start_ref[1] + c + index % WIN
                zr = (row >= total_rows - WIN).astype(jnp.int32) + (
                    row >= total_rows - WIN // 2
                ).astype(jnp.int32)
                zc = (col >= total_cols - WIN).astype(jnp.int32) + (
                    col >= total_cols - WIN // 2
                ).astype(jnp.int32)
                return zr * 3 + zc

            masks.append(zone(0) == zone(1))
    return masks


def attend(q_stack, k, position, mask, scale):
    scores = mm_nt(q_stack, k) * scale + position
    if mask is not None:
        scores = jnp.where(mask, scores, -1e30)
    powers = jnp.exp(scores - jnp.max(scores, axis=-1, keepdims=True))
    return powers / jnp.sum(powers, axis=-1, keepdims=True)


def forward(x, w, position, masks, heads):
    cells = WIN * WIN
    channels = x.shape[1]
    size = channels // heads
    unit, _ = norm_parts(x)
    normed = (unit * w["ng"][...] + w["nb"][...]).astype(BF16)
    packed = (mm(normed, w["wqkv"][0]) + w["bqkv"][...]).astype(BF16)
    hmask = head_rows(cells, heads, size)
    mixed = []
    for n in range(x.shape[0] // cells):
        at = slice(n * cells, (n + 1) * cells)
        q = packed[at, :channels]
        k = packed[at, channels : 2 * channels]
        v = packed[at, 2 * channels :]
        probs = attend(
            spread_heads(q, hmask, heads), k, position, None if masks is None else masks[n],
            size ** (-0.5),
        )
        mixed.append(fold_heads(mm(probs.astype(BF16), v), hmask, heads, cells).astype(BF16))
    mixed = jnp.concatenate(mixed, axis=0)
    mid = (x + mm(mixed, w["wproj"][0]) + w["bproj"][...]).astype(BF16)
    mid32 = mid.astype(F32)
    unit2, _ = norm_parts(mid32)
    normed2 = (unit2 * w["mg"][...] + w["mb"][...]).astype(BF16)
    pre = mm(normed2, w["wup"][0]) + w["bup"][...]
    half = 0.5 * (1.0 + lax.erf(pre * (2.0**-0.5)))
    hidden = (pre * half).astype(BF16)
    out = (mid32 + mm(hidden, w["wdown"][0]) + w["bdown"][...]).astype(BF16)
    return out, (packed, mixed, mid, pre)


def backward(x, g, saved, w, position, masks, heads, grads_ref, light_ref):
    packed, mixed, mid, pre = saved
    cells = WIN * WIN
    channels = x.shape[1]
    size = channels // heads
    scale = size ** (-0.5)
    light_ref[...] = jnp.zeros_like(light_ref)
    g16 = g.astype(BF16)
    half = 0.5 * (1.0 + lax.erf(pre * (2.0**-0.5)))
    slope = half + pre * jnp.exp(-0.5 * pre * pre) * 0.3989422804014327
    hidden = (pre * half).astype(BF16)
    grads_ref[2 * channels : 3 * channels, :] = mm_tn(g16, hidden).astype(BF16)
    light_ref[3:4, :channels] = jnp.sum(g, axis=0, keepdims=True)
    dpre = rnd(mm_nt(g16, w["wdown"][0])) * slope
    light_ref[0:1, : dpre.shape[1]] = jnp.sum(dpre, axis=0, keepdims=True)
    dpre16 = dpre.astype(BF16)
    mid32 = mid.astype(F32)
    unit2, inv2 = norm_parts(mid32)
    normed2 = (unit2 * w["mg"][...] + w["mb"][...]).astype(BF16)
    grads_ref[channels : 2 * channels, :] = mm_tn(normed2, dpre16).astype(BF16)
    dn2 = rnd(mm_nt(dpre16, w["wup"][0]))
    light_ref[2:3, 2 * channels : 3 * channels] = jnp.sum(dn2 * unit2, axis=0, keepdims=True)
    light_ref[2:3, 3 * channels : 4 * channels] = jnp.sum(dn2, axis=0, keepdims=True)
    dmid = rnd(rnd(norm_back(unit2, inv2, w["mg"][...], dn2)) + g)
    dmid16 = dmid.astype(BF16)
    light_ref[1:2, 3 * channels : 4 * channels] = jnp.sum(dmid, axis=0, keepdims=True)
    grads_ref[0:channels, 3 * channels : 4 * channels] = mm_tn(mixed, dmid16).astype(BF16)
    dmixed = mm_nt(dmid16, w["wproj"][0]).astype(BF16)
    hmask = head_rows(cells, heads, size)
    dpacked = []
    dposition = None
    for n in range(x.shape[0] // cells):
        at = slice(n * cells, (n + 1) * cells)
        q_stack = spread_heads(packed[at, :channels], hmask, heads)
        k = packed[at, channels : 2 * channels]
        v = packed[at, 2 * channels :]
        probs = attend(q_stack, k, position, None if masks is None else masks[n], scale)
        d_stack = spread_heads(dmixed[at], hmask, heads)
        dprobs = rnd(mm_nt(d_stack, v))
        dv = mm_tn(probs.astype(BF16), d_stack)
        ds = probs * (dprobs - jnp.sum(probs * dprobs, axis=-1, keepdims=True))
        dposition = ds if dposition is None else dposition + ds
        ds16 = (ds * scale).astype(BF16)
        dq = fold_heads(mm(ds16, k), hmask, heads, cells)
        dk = mm_tn(ds16, q_stack)
        dpacked.append(jnp.concatenate([dq, dk, dv], axis=1).astype(BF16))
    light_ref[4 : 4 + 12, 0:256] = position_grad(dposition, heads)[:12]
    dpacked = jnp.concatenate(dpacked, axis=0)
    light_ref[1:2, : 3 * channels] = jnp.sum(dpacked.astype(F32), axis=0, keepdims=True)
    unit, inv = norm_parts(x)
    normed = (unit * w["ng"][...] + w["nb"][...]).astype(BF16)
    grads_ref[0:channels, : 3 * channels] = mm_tn(normed, dpacked).astype(BF16)
    dn = rnd(mm_nt(dpacked, w["wqkv"][0]))
    light_ref[2:3, 0:channels] = jnp.sum(dn * unit, axis=0, keepdims=True)
    light_ref[2:3, channels : 2 * channels] = jnp.sum(dn, axis=0, keepdims=True)
    dx = rnd(norm_back(unit, inv, w["ng"][...], dn)) + dmid
    grads_ref[3 * channels : 3 * channels + 16, :] = light_ref[...].astype(BF16)
    rest = grads_ref.shape[0] - 3 * channels - 16
    if rest:
        grads_ref[3 * channels + 16 :, :] = jnp.zeros((rest, grads_ref.shape[1]), BF16)
    return dx


KEYS = ("ng", "nb", "wqkv", "bqkv", "rel", "wproj", "bproj", "mg", "mb", "wup", "bup", "wdown", "bdown")
MATRICES = ("wqkv", "rel", "wproj", "wup", "wdown")


def weight_view(refs, block):
    view = {}
    for key, ref in zip(KEYS, refs):
        view[key] = ref if key in MATRICES else ref.at[block : block + 1, :]
    return view


def weight_specs(params, block):
    specs = []
    for key, member in zip(KEYS, params):
        if key in MATRICES:
            specs.append(pl.BlockSpec((1,) + member.shape[1:], lambda i: (block, 0, 0)))
        else:
            specs.append(pl.BlockSpec(member.shape, lambda i: (0, 0)))
    return specs


def whole(shape):
    return pl.BlockSpec(shape, lambda i: (0,) * len(shape))


def shape_of(shape, dtype):
    return jax.ShapeDtypeStruct(shape, dtype)


def first_forward(imagery, params):
    height, breadth, channels = imagery.shape
    heads = params[4].shape[1]
    tokens = height * breadth
    mlp = params[9].shape[2]

    def body(x_ref, *refs):
        w = weight_view(refs[: len(KEYS)], 0)
        out_ref, packed_ref, mixed_ref, mid_ref, pre_ref, pos_ref = refs[len(KEYS) :]
        x = load_windows(x_ref, height, breadth)
        position = position_stack(w["rel"][0], heads)
        pos_ref[...] = position
        out, saved = forward(x, w, position, None, heads)
        store_windows(out_ref, out.astype(F32), height, breadth)
        for ref, value in zip((packed_ref, mixed_ref, mid_ref, pre_ref), saved):
            ref[...] = value

    outs = [
        shape_of(imagery.shape, BF16),
        shape_of((tokens, 3 * channels), BF16),
        shape_of((tokens, channels), BF16),
        shape_of((tokens, channels), BF16),
        shape_of((tokens, mlp), F32),
        shape_of((heads * WIN * WIN, WIN * WIN), F32),
    ]
    return pl.pallas_call(
        body,
        name="fwd0",
        grid=(1,),
        out_shape=outs,
        in_specs=[whole(imagery.shape)] + weight_specs(params, 0),
        out_specs=[whole(o.shape) for o in outs],
    )(imagery, *params)


def second_both(moved, grad, start, params, total_rows, total_cols, grad_rows):
    height, breadth, channels = moved.shape
    heads = params[4].shape[1]
    width = params[9].shape[2]

    def body(start_ref, x_ref, g_ref, *refs):
        w = weight_view(refs[: len(KEYS)], 1)
        out_ref, dx_ref, grads_ref, light_ref = refs[len(KEYS) :]
        x = load_windows(x_ref, height, breadth)
        position = position_stack(w["rel"][0], heads)
        masks = zone_masks(start_ref, height, breadth, total_rows, total_cols, heads)
        out, saved = forward(x, w, position, masks, heads)
        store_windows(out_ref, out.astype(F32), height, breadth)
        g = load_windows(g_ref, height, breadth)
        dx = backward(x, g, saved, w, position, masks, heads, grads_ref, light_ref)
        store_windows(dx_ref, dx, height, breadth)

    outs = [
        shape_of(moved.shape, BF16),
        shape_of(moved.shape, BF16),
        shape_of((grad_rows, width), BF16),
    ]
    return pl.pallas_call(
        body,
        name="both1",
        grid=(1,),
        out_shape=outs,
        in_specs=[pl.BlockSpec(memory_space=pltpu.SMEM), whole(moved.shape), whole(moved.shape)]
        + weight_specs(params, 1),
        out_specs=[whole(o.shape) for o in outs],
        scratch_shapes=[pltpu.VMEM((16, width), F32)],
    )(start, moved, grad, *params)


def first_backward(imagery, grad, saved, params, grad_rows):
    height, breadth, channels = imagery.shape
    heads = params[4].shape[1]
    width = params[9].shape[2]

    def body(x_ref, g_ref, packed_ref, mixed_ref, mid_ref, pre_ref, pos_ref, *refs):
        w = weight_view(refs[: len(KEYS)], 0)
        dx_ref, grads_ref, light_ref = refs[len(KEYS) :]
        x = load_windows(x_ref, height, breadth)
        g = load_windows(g_ref, height, breadth)
        values = (packed_ref[...], mixed_ref[...], mid_ref[...], pre_ref[...])
        dx = backward(x, g, values, w, pos_ref[...], None, heads, grads_ref, light_ref)
        store_windows(dx_ref, dx, height, breadth)

    outs = [shape_of(imagery.shape, BF16), shape_of((grad_rows, width), BF16)]
    return pl.pallas_call(
        body,
        name="bwd0",
        grid=(1,),
        out_shape=outs,
        in_specs=[whole(imagery.shape), whole(grad.shape)]
        + [whole(s.shape) for s in saved]
        + weight_specs(params, 0),
        out_specs=[whole(o.shape) for o in outs],
        scratch_shapes=[pltpu.VMEM((16, width), F32)],
    )(imagery, grad, *saved, *params)


def sum_all(grads_one, grads_two, nz, nq):
    block_rows, width = grads_one.shape
    rows = 2 * block_rows
    half = width // 2
    part = rows // nq
    piece = part // nz

    def body(one_ref, two_ref, out_ref, buf0, acc, buf1, acc1, buf2, send, recv):
        z = lax.axis_index("rows")
        col = lax.axis_index("cols")
        core = lax.rem(col, 2)
        q = col // 2
        mine = pl.multiple_of(core * half, 128)
        other = pl.multiple_of((1 - core) * half, 128)
        partner = (z, q * 2 + (1 - core))
        across = [(z, lax.rem(q + d, nq) * 2 + core) for d in range(1, nq)]
        along = [(lax.rem(z + d, nz), col) for d in range(1, nz)]
        barrier = pltpu.get_barrier_semaphore()
        for peer in [partner] + across + along:
            pl.semaphore_signal(barrier, inc=1, device_id=peer, device_id_type=MESH)
        pl.semaphore_wait(barrier, nq + nz - 1)

        def copy(src, dst, index, peer):
            c = pltpu.make_async_remote_copy(
                src_ref=src,
                dst_ref=dst,
                send_sem=send.at[index],
                recv_sem=recv.at[index],
                device_id=peer,
                device_id_type=MESH,
            )
            c.start()
            return c

        sem = 0
        copies = []
        for b, ref in enumerate((one_ref, two_ref)):
            copies.append(
                copy(ref.at[:, pl.ds(other, half)], buf0.at[pl.ds(b * block_rows, block_rows), :], sem, partner)
            )
            sem += 1
        for b, ref in enumerate((one_ref, two_ref)):
            copies[b].wait()
            at = pl.ds(b * block_rows, block_rows)
            acc[at, :] = (ref[:, pl.ds(mine, half)].astype(F32) + buf0[at, :].astype(F32)).astype(BF16)
        copies = []
        for d in range(1, nq):
            to = pl.multiple_of(lax.rem(q + d, nq) * part, 16)
            copies.append(copy(acc.at[pl.ds(to, part), :], buf1.at[d - 1], sem, across[d - 1]))
            sem += 1
        total = acc[pl.ds(pl.multiple_of(q * part, 16), part), :].astype(F32)
        for d in range(1, nq):
            copies[d - 1].wait()
            total = total + buf1[d - 1].astype(F32)
        acc1[...] = total.astype(BF16)
        copies = []
        for d in range(1, nz):
            to = pl.multiple_of(lax.rem(z + d, nz) * piece, 16)
            copies.append(copy(acc1.at[pl.ds(to, piece), :], buf2.at[d - 1], sem, along[d - 1]))
            sem += 1
        total = acc1[pl.ds(pl.multiple_of(z * piece, 16), piece), :].astype(F32)
        for d in range(1, nz):
            copies[d - 1].wait()
            total = total + buf2[d - 1].astype(F32)
        lanes = pl.ds(mine, half)
        own = pl.ds(pl.multiple_of(q * part + z * piece, 16), piece)
        out_ref[own, lanes] = total.astype(BF16)
        copies = []
        for d in range(1, nz):
            copies.append(copy(out_ref.at[own, lanes], out_ref.at[own, lanes], sem, along[d - 1]))
            sem += 1
        for c in copies:
            c.wait()
        copies = []
        own = pl.ds(pl.multiple_of(q * part, 16), part)
        for d in range(1, nq):
            copies.append(copy(out_ref.at[own, lanes], out_ref.at[own, lanes], sem, across[d - 1]))
            sem += 1
        for c in copies:
            c.wait()
        copy(out_ref.at[:, lanes], out_ref.at[:, lanes], sem, partner).wait()

    sems = 2 + 2 * (nq - 1) + 2 * (nz - 1) + 1
    vmem = pl.BlockSpec(memory_space=pltpu.VMEM)
    return pl.pallas_call(
        body,
        name="sum_all",
        out_shape=shape_of((rows, width), BF16),
        in_specs=[vmem, vmem],
        out_specs=vmem,
        scratch_shapes=[
            pltpu.VMEM((rows, half), BF16),
            pltpu.VMEM((rows, half), BF16),
            pltpu.VMEM((max(nq - 1, 1), part, half), BF16),
            pltpu.VMEM((part, half), BF16),
            pltpu.VMEM((max(nz - 1, 1), piece, half), BF16),
            pltpu.SemaphoreType.DMA((sems,)),
            pltpu.SemaphoreType.DMA((sems,)),
        ],
        compiler_params=pltpu.CompilerParams(collective_id=0, has_side_effects=True),
    )(grads_one, grads_two)


def unpack(summed, params, factor):
    channels = params[0].shape[1]
    heads, offsets = params[4].shape[1:]
    block_rows = summed.shape[0] // 2

    def body(s_ref, *outs):
        o = dict(zip(KEYS, outs))
        for b in range(2):
            at = b * block_rows

            def rows(low, count):
                return s_ref[at + low : at + low + count, :].astype(F32) * factor

            top = rows(0, channels)
            o["wqkv"][b] = top[:, : 3 * channels]
            o["wproj"][b] = top[:, 3 * channels :]
            o["wup"][b] = rows(channels, channels)
            o["wdown"][b] = rows(2 * channels, channels).T
            light = rows(3 * channels, 16)
            o["bup"][b : b + 1, :] = light[0:1, :]
            o["bqkv"][b : b + 1, :] = light[1:2, : 3 * channels]
            o["bproj"][b : b + 1, :] = light[1:2, 3 * channels :]
            for place, key in enumerate(("ng", "nb", "mg", "mb")):
                o[key][b : b + 1, :] = light[2:3, place * channels : (place + 1) * channels]
            o["bdown"][b : b + 1, :] = light[3:4, :channels]
            o["rel"][b] = light[4 : 4 + heads, :offsets]

    outs = [shape_of(member.shape, F32) for member in params]
    return pl.pallas_call(
        body,
        name="unpack",
        grid=(1,),
        out_shape=outs,
        in_specs=[whole(summed.shape)],
        out_specs=[whole(o.shape) for o in outs],
    )(summed)


def from_behind(value, axis, steps):
    count = lax.axis_size(axis)
    pairs = [(source, (source + steps) % count) for source in range(count)]
    return lax.ppermute(value, axis, pairs)


def along_axis(values, axis, name, direction):
    half = WIN // 2
    size = values.shape[axis]
    if direction < 0:
        outgoing = lax.slice_in_dim(values, 0, half, axis=axis)
        kept = lax.slice_in_dim(values, half, size, axis=axis)
    else:
        outgoing = lax.slice_in_dim(values, size - half, size, axis=axis)
        kept = lax.slice_in_dim(values, 0, size - half, axis=axis)
    arrived = from_behind(outgoing, name, direction)
    return jnp.concatenate([kept, arrived] if direction < 0 else [arrived, kept], axis=axis)


def advance(values):
    return along_axis(along_axis(values, 0, "rows", -1), 1, "cols", -1)


def retreat(values):
    return along_axis(along_axis(values, 0, "rows", 1), 1, "cols", 1)


def per_device(imagery, cotangent, *params):
    height, breadth, channels = imagery.shape
    nz = lax.axis_size("rows")
    nc = lax.axis_size("cols")
    total_rows = height * nz
    total_cols = breadth * nc
    start = jnp.stack(
        [lax.axis_index("rows") * height, lax.axis_index("cols") * breadth]
    ).astype(jnp.int32)
    unit = nz * (nc // 2) * 8
    grad_rows = -(-(3 * channels + 16) // unit) * unit
    level_one, *saved = first_forward(imagery, params)
    level_two, back_two, grads_two = second_both(
        advance(level_one), advance(cotangent), start, params, total_rows, total_cols, grad_rows
    )
    output = retreat(level_two)
    back_one, grads_one = first_backward(imagery, retreat(back_two), saved, params, grad_rows)
    summed = sum_all(grads_one, grads_two, nz, nc // 2)
    merged = unpack(summed, params, float(total_rows * total_cols) ** (-0.5))
    return (output, back_one) + tuple(merged)


def solution(mesh):
    tile = P("rows", "cols", None)
    return jax.shard_map(
        per_device,
        mesh=mesh,
        in_specs=(tile, tile) + (P(),) * 13,
        out_specs=(tile, tile) + (P(),) * 13,
        check_vma=False,
    )
```

```python
import functools

import jax
import jax.numpy as jnp
from jax import lax
from jax.experimental import pallas as pl
from jax.experimental.pallas import tpu as pltpu
from jax.sharding import PartitionSpec as P

WIN = 8
EPSILON = 1e-05
F32 = jnp.float32
BF16 = jnp.bfloat16
MESH = pl.DeviceIdType.MESH


def mm(a, b):
    return jnp.dot(a, b, preferred_element_type=F32)


def mm_nt(a, b):
    return lax.dot_general(a, b, (((1,), (1,)), ((), ())), preferred_element_type=F32)


def mm_tn(a, b):
    return lax.dot_general(a, b, (((0,), (0,)), ((), ())), preferred_element_type=F32)


def split3(x):
    hi = x.astype(BF16)
    rest = x - hi.astype(F32)
    mid = rest.astype(BF16)
    return hi, mid, (rest - mid.astype(F32)).astype(BF16)


def load_windows(ref, height, breadth):
    parts = []
    for r in range(0, height, WIN):
        for c in range(0, breadth, WIN):
            piece = ref[r : r + WIN, c : c + WIN, :].astype(F32)
            parts.append(piece.reshape(WIN * WIN, piece.shape[-1]))
    return jnp.concatenate(parts, axis=0)


def store_windows(ref, values, height, breadth):
    at = 0
    for r in range(0, height, WIN):
        for c in range(0, breadth, WIN):
            piece = values[at : at + WIN * WIN].reshape(WIN, WIN, values.shape[-1])
            ref[r : r + WIN, c : c + WIN, :] = piece.astype(ref.dtype)
            at += WIN * WIN


def norm_parts(x):
    center = x - jnp.mean(x, axis=-1, keepdims=True)
    spread = jnp.mean(center * center, axis=-1, keepdims=True)
    inv = lax.rsqrt(spread + EPSILON)
    return center * inv, inv


def norm_back(unit, inv, gain, grad):
    scaled = grad * gain
    m1 = jnp.mean(scaled, axis=-1, keepdims=True)
    m2 = jnp.mean(scaled * unit, axis=-1, keepdims=True)
    return inv * (scaled - m1 - unit * m2)


def rnd(x):
    return x.astype(BF16).astype(F32)


def head_rows(rows, heads, size):
    lane = lax.broadcasted_iota(jnp.int32, (heads * rows, heads * size), 1)
    row = lax.broadcasted_iota(jnp.int32, (heads * rows, heads * size), 0)
    return (lane // size) == (row // rows)


def spread_heads(x, mask, heads):
    tiled = jnp.concatenate([x] * heads, axis=0)
    return jnp.where(mask, tiled, jnp.zeros_like(tiled))


def fold_heads(x, mask, heads, rows):
    kept = jnp.where(mask, x, 0.0)
    total = kept[:rows]
    for h in range(1, heads):
        total = total + kept[h * rows : (h + 1) * rows]
    return total


def cell_code(n, dim, shape):
    index = lax.broadcasted_iota(jnp.int32, shape, dim)
    return (index // WIN) * (2 * WIN - 1) + index % WIN


def position_stack(rel, heads):
    cells = WIN * WIN
    span = 2 * WIN - 1
    middle = (span * span - 1) // 2
    width = 256
    lanes = lax.broadcasted_iota(jnp.int32, (cells, 128), 1)
    pick = (lanes == cell_code(cells, 0, (cells, 128))).astype(BF16)
    outs = []
    for h in range(heads):
        row = jnp.concatenate([rel[h], jnp.zeros((1, width - span * span), F32)], axis=1)
        row = jnp.broadcast_to(row, (WIN, width))
        rolled = [
            pltpu.roll(row, (span * y - middle) % width, 1, stride=1, stride_axis=0)[:, :128]
            for y in range(WIN)
        ]
        parts = split3(jnp.concatenate(rolled, axis=0))
        outs.append(mm_nt(pick, parts[0]) + mm_nt(pick, parts[1]) + mm_nt(pick, parts[2]))
    return jnp.concatenate(outs, axis=0)


def position_grad(dstack, heads):
    cells = WIN * WIN
    span = 2 * WIN - 1
    middle = (span * span - 1) // 2
    width = 256
    lanes = lax.broadcasted_iota(jnp.int32, (cells, width), 1)
    pick = (lanes == middle - cell_code(cells, 0, (cells, width))).astype(BF16)
    rows = []
    for h in range(heads):
        hi, mid, _ = split3(dstack[h * cells : (h + 1) * cells])
        flipped = mm_tn(hi, pick) + mm_tn(mid, pick)
        total = None
        for y in range(WIN):
            part = pltpu.roll(
                flipped[y * WIN : (y + 1) * WIN], span * y, 1, stride=1, stride_axis=0
            )
            total = part if total is None else total + part
        rows.append(jnp.sum(total, axis=0, keepdims=True))
    rows.append(jnp.zeros((16 - heads, width), F32))
    stacked = jnp.concatenate(rows, axis=0)
    back = (
        lax.broadcasted_iota(jnp.int32, (width, width), 0)
        + lax.broadcasted_iota(jnp.int32, (width, width), 1)
        == span * span - 1
    ).astype(BF16)
    hi, mid, _ = split3(stacked)
    return mm(hi, back) + mm(mid, back)


def zone_masks(start_ref, height, breadth, total_rows, total_cols, heads):
    cells = WIN * WIN
    masks = []
    for r in range(0, height, WIN):
        for c in range(0, breadth, WIN):

            def zone(dim):
                index = lax.broadcasted_iota(jnp.int32, (heads * cells, cells), dim) % cells
                row = start_ref[0] + r + index // WIN
                col = start_ref[1] + c + index % WIN
                zr = (row >= total_rows - WIN).astype(jnp.int32) + (
                    row >= total_rows - WIN // 2
                ).astype(jnp.int32)
                zc = (col >= total_cols - WIN).astype(jnp.int32) + (
                    col >= total_cols - WIN // 2
                ).astype(jnp.int32)
                return zr * 3 + zc

            masks.append(zone(0) == zone(1))
    return masks


def attend(q_stack, k, position, mask, scale):
    scores = mm_nt(q_stack, k) * scale + position
    if mask is not None:
        scores = jnp.where(mask, scores, -1e30)
    powers = jnp.exp(scores - jnp.max(scores, axis=-1, keepdims=True))
    return powers / jnp.sum(powers, axis=-1, keepdims=True)


def forward(x, w, position, masks, heads):
    cells = WIN * WIN
    channels = x.shape[1]
    size = channels // heads
    unit, _ = norm_parts(x)
    normed = (unit * w["ng"][...] + w["nb"][...]).astype(BF16)
    packed = (mm(normed, w["wqkv"][0]) + w["bqkv"][...]).astype(BF16)
    hmask = head_rows(cells, heads, size)
    mixed = []
    for n in range(x.shape[0] // cells):
        at = slice(n * cells, (n + 1) * cells)
        q = packed[at, :channels]
        k = packed[at, channels : 2 * channels]
        v = packed[at, 2 * channels :]
        probs = attend(
            spread_heads(q, hmask, heads), k, position, None if masks is None else masks[n],
            size ** (-0.5),
        )
        mixed.append(fold_heads(mm(probs.astype(BF16), v), hmask, heads, cells).astype(BF16))
    mixed = jnp.concatenate(mixed, axis=0)
    mid = (x + mm(mixed, w["wproj"][0]) + w["bproj"][...]).astype(BF16)
    mid32 = mid.astype(F32)
    unit2, _ = norm_parts(mid32)
    normed2 = (unit2 * w["mg"][...] + w["mb"][...]).astype(BF16)
    pre = mm(normed2, w["wup"][0]) + w["bup"][...]
    half = 0.5 * (1.0 + lax.erf(pre * (2.0**-0.5)))
    hidden = (pre * half).astype(BF16)
    out = (mid32 + mm_nt(hidden, w["wdown"][0]) + w["bdown"][...]).astype(BF16)
    return out, (packed, mixed, mid, pre)


def backward(x, g, saved, w, position, masks, heads, grads_ref, light_ref):
    packed, mixed, mid, pre = saved
    cells = WIN * WIN
    channels = x.shape[1]
    size = channels // heads
    scale = size ** (-0.5)
    light_ref[...] = jnp.zeros_like(light_ref)
    g16 = g.astype(BF16)
    half = 0.5 * (1.0 + lax.erf(pre * (2.0**-0.5)))
    slope = half + pre * jnp.exp(-0.5 * pre * pre) * 0.3989422804014327
    hidden = (pre * half).astype(BF16)
    grads_ref[2 * channels : 3 * channels, :] = mm_tn(g16, hidden).astype(BF16)
    light_ref[3:4, :channels] = jnp.sum(g, axis=0, keepdims=True)
    dpre = rnd(mm(g16, w["wdown"][0])) * slope
    light_ref[0:1, : dpre.shape[1]] = jnp.sum(dpre, axis=0, keepdims=True)
    dpre16 = dpre.astype(BF16)
    mid32 = mid.astype(F32)
    unit2, inv2 = norm_parts(mid32)
    normed2 = (unit2 * w["mg"][...] + w["mb"][...]).astype(BF16)
    grads_ref[channels : 2 * channels, :] = mm_tn(normed2, dpre16).astype(BF16)
    dn2 = rnd(mm_nt(dpre16, w["wup"][0]))
    light_ref[2:3, 2 * channels : 3 * channels] = jnp.sum(dn2 * unit2, axis=0, keepdims=True)
    light_ref[2:3, 3 * channels : 4 * channels] = jnp.sum(dn2, axis=0, keepdims=True)
    dmid = rnd(rnd(norm_back(unit2, inv2, w["mg"][...], dn2)) + g)
    dmid16 = dmid.astype(BF16)
    light_ref[1:2, 3 * channels : 4 * channels] = jnp.sum(dmid, axis=0, keepdims=True)
    grads_ref[0:channels, 3 * channels : 4 * channels] = mm_tn(mixed, dmid16).astype(BF16)
    dmixed = mm_nt(dmid16, w["wproj"][0]).astype(BF16)
    hmask = head_rows(cells, heads, size)
    dpacked = []
    dposition = None
    for n in range(x.shape[0] // cells):
        at = slice(n * cells, (n + 1) * cells)
        q_stack = spread_heads(packed[at, :channels], hmask, heads)
        k = packed[at, channels : 2 * channels]
        v = packed[at, 2 * channels :]
        probs = attend(q_stack, k, position, None if masks is None else masks[n], scale)
        d_stack = spread_heads(dmixed[at], hmask, heads)
        dprobs = rnd(mm_nt(d_stack, v))
        dv = mm_tn(probs.astype(BF16), d_stack)
        ds = probs * (dprobs - jnp.sum(probs * dprobs, axis=-1, keepdims=True))
        dposition = ds if dposition is None else dposition + ds
        ds16 = (ds * scale).astype(BF16)
        dq = fold_heads(mm(ds16, k), hmask, heads, cells)
        dk = mm_tn(ds16, q_stack)
        dpacked.append(jnp.concatenate([dq, dk, dv], axis=1).astype(BF16))
    light_ref[4 : 4 + 12, 0:256] = position_grad(dposition, heads)[:12]
    dpacked = jnp.concatenate(dpacked, axis=0)
    light_ref[1:2, : 3 * channels] = jnp.sum(dpacked.astype(F32), axis=0, keepdims=True)
    unit, inv = norm_parts(x)
    normed = (unit * w["ng"][...] + w["nb"][...]).astype(BF16)
    grads_ref[0:channels, : 3 * channels] = mm_tn(normed, dpacked).astype(BF16)
    dn = rnd(mm_nt(dpacked, w["wqkv"][0]))
    light_ref[2:3, 0:channels] = jnp.sum(dn * unit, axis=0, keepdims=True)
    light_ref[2:3, channels : 2 * channels] = jnp.sum(dn, axis=0, keepdims=True)
    dx = rnd(norm_back(unit, inv, w["ng"][...], dn)) + dmid
    grads_ref[3 * channels : 3 * channels + 16, :] = light_ref[...].astype(BF16)
    rest = grads_ref.shape[0] - 3 * channels - 16
    if rest:
        grads_ref[3 * channels + 16 :, :] = jnp.zeros((rest, grads_ref.shape[1]), BF16)
    return dx


KEYS = ("ng", "nb", "wqkv", "bqkv", "rel", "wproj", "bproj", "mg", "mb", "wup", "bup", "wdown", "bdown")
MATRICES = ("wqkv", "wproj", "wup", "wdown")


def weight_view(refs, block):
    view = {}
    for key, ref in zip(KEYS, refs):
        if key == "rel":
            view[key] = [ref[h, block : block + 1, :] for h in range(ref.shape[0])]
        else:
            view[key] = ref if key in MATRICES else ref.at[block : block + 1, :]
    return view


def weight_specs(params, block):
    specs = []
    for key, member in zip(KEYS, params):
        if key in MATRICES:
            specs.append(pl.BlockSpec((1,) + member.shape[1:], lambda i: (block, 0, 0)))
        else:
            specs.append(whole(member.shape))
    return specs


def whole(shape):
    return pl.BlockSpec(shape, lambda i: (0,) * len(shape))


def shape_of(shape, dtype):
    return jax.ShapeDtypeStruct(shape, dtype)


def first_forward(imagery, params):
    height, breadth, channels = imagery.shape
    heads = params[4].shape[0]
    tokens = height * breadth
    mlp = params[9].shape[2]

    def body(x_ref, *refs):
        w = weight_view(refs[: len(KEYS)], 0)
        out_ref, packed_ref, mixed_ref, mid_ref, pre_ref, pos_ref = refs[len(KEYS) :]
        x = load_windows(x_ref, height, breadth)
        position = position_stack(w["rel"], heads)
        pos_ref[...] = position
        out, saved = forward(x, w, position, None, heads)
        store_windows(out_ref, out.astype(F32), height, breadth)
        for ref, value in zip((packed_ref, mixed_ref, mid_ref, pre_ref), saved):
            ref[...] = value

    outs = [
        shape_of(imagery.shape, BF16),
        shape_of((tokens, 3 * channels), BF16),
        shape_of((tokens, channels), BF16),
        shape_of((tokens, channels), BF16),
        shape_of((tokens, mlp), F32),
        shape_of((heads * WIN * WIN, WIN * WIN), F32),
    ]
    return pl.pallas_call(
        body,
        name="fwd0",
        grid=(1,),
        out_shape=outs,
        in_specs=[whole(imagery.shape)] + weight_specs(params, 0),
        out_specs=[whole(o.shape) for o in outs],
    )(imagery, *params)


def second_both(moved, grad, start, params, total_rows, total_cols, grad_rows):
    height, breadth, channels = moved.shape
    heads = params[4].shape[0]
    width = params[9].shape[2]

    def body(start_ref, x_ref, g_ref, *refs):
        w = weight_view(refs[: len(KEYS)], 1)
        out_ref, dx_ref, grads_ref, light_ref = refs[len(KEYS) :]
        x = load_windows(x_ref, height, breadth)
        position = position_stack(w["rel"], heads)
        masks = zone_masks(start_ref, height, breadth, total_rows, total_cols, heads)
        out, saved = forward(x, w, position, masks, heads)
        store_windows(out_ref, out.astype(F32), height, breadth)
        g = load_windows(g_ref, height, breadth)
        dx = backward(x, g, saved, w, position, masks, heads, grads_ref, light_ref)
        store_windows(dx_ref, dx, height, breadth)

    outs = [
        shape_of(moved.shape, BF16),
        shape_of(moved.shape, BF16),
        shape_of((grad_rows, width), BF16),
    ]
    return pl.pallas_call(
        body,
        name="both1",
        grid=(1,),
        out_shape=outs,
        in_specs=[pl.BlockSpec(memory_space=pltpu.SMEM), whole(moved.shape), whole(moved.shape)]
        + weight_specs(params, 1),
        out_specs=[whole(o.shape) for o in outs],
        scratch_shapes=[pltpu.VMEM((16, width), F32)],
    )(start, moved, grad, *params)


def first_backward(imagery, grad, saved, params, grad_rows):
    height, breadth, channels = imagery.shape
    heads = params[4].shape[0]
    width = params[9].shape[2]

    def body(x_ref, g_ref, packed_ref, mixed_ref, mid_ref, pre_ref, pos_ref, *refs):
        w = weight_view(refs[: len(KEYS)], 0)
        dx_ref, grads_ref, light_ref = refs[len(KEYS) :]
        x = load_windows(x_ref, height, breadth)
        g = load_windows(g_ref, height, breadth)
        values = (packed_ref[...], mixed_ref[...], mid_ref[...], pre_ref[...])
        dx = backward(x, g, values, w, pos_ref[...], None, heads, grads_ref, light_ref)
        store_windows(dx_ref, dx, height, breadth)

    outs = [shape_of(imagery.shape, BF16), shape_of((grad_rows, width), BF16)]
    return pl.pallas_call(
        body,
        name="bwd0",
        grid=(1,),
        out_shape=outs,
        in_specs=[whole(imagery.shape), whole(grad.shape)]
        + [whole(s.shape) for s in saved]
        + weight_specs(params, 0),
        out_specs=[whole(o.shape) for o in outs],
        scratch_shapes=[pltpu.VMEM((16, width), F32)],
    )(imagery, grad, *saved, *params)


def sum_all(grads_one, grads_two, nz, nq):
    block_rows, width = grads_one.shape
    rows = 2 * block_rows
    half = width // 2
    unit = nq * nz * 16
    count = rows // unit
    part = unit // nq
    piece = 16
    per_chunk = 2 * nq + 2 * nz - 1

    def body(one_ref, two_ref, out_ref, buf0, acc, buf1, acc1, buf2, send, recv):
        z = lax.axis_index("rows")
        col = lax.axis_index("cols")
        core = lax.rem(col, 2)
        q = col // 2
        mine = pl.multiple_of(core * half, 128)
        other = pl.multiple_of((1 - core) * half, 128)
        partner = (z, q * 2 + (1 - core))
        across = [(z, lax.rem(q + d, nq) * 2 + core) for d in range(1, nq)]
        along = [(lax.rem(z + d, nz), col) for d in range(1, nz)]
        barrier = pltpu.get_barrier_semaphore()
        for peer in [partner] + across + along:
            pl.semaphore_signal(barrier, inc=1, device_id=peer, device_id_type=MESH)
        pl.semaphore_wait(barrier, nq + nz - 1)
        lanes = pl.ds(mine, half)
        pending = {}

        def copy(chunk, slot, src, dst, peer):
            index = chunk * per_chunk + slot
            c = pltpu.make_async_remote_copy(
                src_ref=src,
                dst_ref=dst,
                send_sem=send.at[index],
                recv_sem=recv.at[index],
                device_id=peer,
                device_id_type=MESH,
            )
            c.start()
            pending.setdefault(chunk, []).append(c)

        def finish(chunk):
            for c in pending.pop(chunk):
                c.wait()

        def pieces(chunk):
            low, high = chunk * unit, (chunk + 1) * unit
            found = []
            for b, ref in ((1, two_ref), (0, one_ref)):
                base = (1 - b) * block_rows
                lo, hi = max(low, base), min(high, base + block_rows)
                if lo < hi:
                    found.append((ref, lo - base, lo - low, hi - lo))
            return found

        def stage0(c):
            for place, (ref, at, to, size) in enumerate(pieces(c)):
                copy(
                    c,
                    place,
                    ref.at[at : at + size, pl.ds(other, half)],
                    buf0.at[c * unit + to : c * unit + to + size, :],
                    partner,
                )

        def stage1(c):
            finish(c)
            for ref, at, to, size in pieces(c):
                where = slice(c * unit + to, c * unit + to + size)
                acc[where, :] = (
                    ref[at : at + size, lanes].astype(F32) + buf0[where, :].astype(F32)
                ).astype(BF16)
            for d in range(1, nq):
                to = pl.multiple_of(c * unit + lax.rem(q + d, nq) * part, 16)
                copy(c, 1 + d, acc.at[pl.ds(to, part), :], buf1.at[c, d - 1], across[d - 1])

        def stage2(c):
            finish(c)
            total = acc[pl.ds(pl.multiple_of(c * unit + q * part, 16), part), :].astype(F32)
            for d in range(1, nq):
                total = total + buf1[c, d - 1].astype(F32)
            acc1[c] = total.astype(BF16)
            for d in range(1, nz):
                to = pl.multiple_of(lax.rem(z + d, nz) * piece, 16)
                copy(c, nq + d, acc1.at[c, pl.ds(to, piece), :], buf2.at[c, d - 1], along[d - 1])

        def stage3(c):
            finish(c)
            total = acc1[c, pl.ds(pl.multiple_of(z * piece, 16), piece), :].astype(F32)
            for d in range(1, nz):
                total = total + buf2[c, d - 1].astype(F32)
            own = pl.ds(pl.multiple_of(c * unit + q * part + z * piece, 16), piece)
            out_ref[own, lanes] = total.astype(BF16)
            for d in range(1, nz):
                copy(c, nq + nz - 1 + d, out_ref.at[own, lanes], out_ref.at[own, lanes], along[d - 1])

        def stage4(c):
            finish(c)
            own = pl.ds(pl.multiple_of(c * unit + q * part, 16), part)
            for d in range(1, nq):
                copy(c, nq + 2 * nz - 2 + d, out_ref.at[own, lanes], out_ref.at[own, lanes], across[d - 1])

        def stage5(c):
            finish(c)
            own = slice(c * unit, (c + 1) * unit)
            copy(c, 2 * nq + 2 * nz - 2, out_ref.at[own, lanes], out_ref.at[own, lanes], partner)

        stages = (stage1, stage2, stage3, stage4, stage5, finish)
        for c in range(count):
            stage0(c)
        for tick in range(count + len(stages) - 1):
            for c in range(count):
                if 0 <= tick - c < len(stages):
                    stages[tick - c](c)

    sems = per_chunk * count
    vmem = pl.BlockSpec(memory_space=pltpu.VMEM)
    return pl.pallas_call(
        body,
        name="sum_all",
        out_shape=shape_of((rows, width), BF16),
        in_specs=[vmem, vmem],
        out_specs=vmem,
        scratch_shapes=[
            pltpu.VMEM((rows, half), BF16),
            pltpu.VMEM((rows, half), BF16),
            pltpu.VMEM((count, max(nq - 1, 1), part, half), BF16),
            pltpu.VMEM((count, part, half), BF16),
            pltpu.VMEM((count, max(nz - 1, 1), piece, half), BF16),
            pltpu.SemaphoreType.DMA((sems,)),
            pltpu.SemaphoreType.DMA((sems,)),
        ],
        compiler_params=pltpu.CompilerParams(collective_id=0, has_side_effects=True),
    )(grads_one, grads_two)


def unpack(summed, params, factor):
    channels = params[0].shape[1]
    heads, _, offsets = params[4].shape
    block_rows = summed.shape[0] // 2

    def body(s_ref, *outs):
        o = dict(zip(KEYS, outs))
        for b in range(2):
            at = (1 - b) * block_rows

            def rows(low, count):
                return s_ref[at + low : at + low + count, :].astype(F32) * factor

            top = rows(0, channels)
            o["wqkv"][b] = top[:, : 3 * channels]
            o["wproj"][b] = top[:, 3 * channels :]
            o["wup"][b] = rows(channels, channels)
            o["wdown"][b] = rows(2 * channels, channels)
            light = rows(3 * channels, 16)
            o["bup"][b : b + 1, :] = light[0:1, :]
            o["bqkv"][b : b + 1, :] = light[1:2, : 3 * channels]
            o["bproj"][b : b + 1, :] = light[1:2, 3 * channels :]
            for place, key in enumerate(("ng", "nb", "mg", "mb")):
                o[key][b : b + 1, :] = light[2:3, place * channels : (place + 1) * channels]
            o["bdown"][b : b + 1, :] = light[3:4, :channels]
            for h in range(heads):
                o["rel"][h, b : b + 1, :] = light[4 + h : 5 + h, :offsets]

    outs = [shape_of(member.shape, F32) for member in params]
    return pl.pallas_call(
        body,
        name="unpack",
        grid=(1,),
        out_shape=outs,
        in_specs=[whole(summed.shape)],
        out_specs=[whole(o.shape) for o in outs],
    )(summed)


def from_behind(value, axis, steps):
    count = lax.axis_size(axis)
    pairs = [(source, (source + steps) % count) for source in range(count)]
    return lax.ppermute(value, axis, pairs)


def along_axis(values, axis, name, direction):
    half = WIN // 2
    size = values.shape[axis]
    if direction < 0:
        outgoing = lax.slice_in_dim(values, 0, half, axis=axis)
        kept = lax.slice_in_dim(values, half, size, axis=axis)
    else:
        outgoing = lax.slice_in_dim(values, size - half, size, axis=axis)
        kept = lax.slice_in_dim(values, 0, size - half, axis=axis)
    arrived = from_behind(outgoing, name, direction)
    return jnp.concatenate([kept, arrived] if direction < 0 else [arrived, kept], axis=axis)


def advance(values):
    return along_axis(along_axis(values, 0, "rows", -1), 1, "cols", -1)


def retreat(values):
    return along_axis(along_axis(values, 0, "rows", 1), 1, "cols", 1)


def per_device(imagery, cotangent, *params):
    height, breadth, channels = imagery.shape
    nz = lax.axis_size("rows")
    nc = lax.axis_size("cols")
    total_rows = height * nz
    total_cols = breadth * nc
    params = list(params)
    params[4] = jnp.swapaxes(params[4], 0, 1)
    params[11] = jnp.swapaxes(params[11], 1, 2)
    start = jnp.stack(
        [lax.axis_index("rows") * height, lax.axis_index("cols") * breadth]
    ).astype(jnp.int32)
    unit = nz * (nc // 2) * 8
    grad_rows = -(-(3 * channels + 16) // unit) * unit
    level_one, *saved = first_forward(imagery, params)
    level_two, back_two, grads_two = second_both(
        advance(level_one), advance(cotangent), start, params, total_rows, total_cols, grad_rows
    )
    output = retreat(level_two)
    back_one, grads_one = first_backward(imagery, retreat(back_two), saved, params, grad_rows)
    summed = sum_all(grads_one, grads_two, nz, nc // 2)
    merged = unpack(summed, params, float(total_rows * total_cols) ** (-0.5))
    merged = list(merged)
    merged[4] = jnp.swapaxes(merged[4], 0, 1)
    merged[11] = jnp.swapaxes(merged[11], 1, 2)
    return (output, back_one) + tuple(merged)


def solution(mesh):
    tile = P("rows", "cols", None)
    return jax.shard_map(
        per_device,
        mesh=mesh,
        in_specs=(tile, tile) + (P(),) * 13,
        out_specs=(tile, tile) + (P(),) * 13,
        check_vma=False,
    )
```

```python
import functools

import jax
import jax.numpy as jnp
from jax import lax
from jax.experimental import pallas as pl
from jax.experimental.pallas import tpu as pltpu
from jax.sharding import PartitionSpec as P

WIN = 8
EPSILON = 1e-05
F32 = jnp.float32
BF16 = jnp.bfloat16
MESH = pl.DeviceIdType.MESH


def mm(a, b):
    return jnp.dot(a, b, preferred_element_type=F32)


def mm_nt(a, b):
    return lax.dot_general(a, b, (((1,), (1,)), ((), ())), preferred_element_type=F32)


def mm_tn(a, b):
    return lax.dot_general(a, b, (((0,), (0,)), ((), ())), preferred_element_type=F32)


def split3(x):
    hi = x.astype(BF16)
    rest = x - hi.astype(F32)
    mid = rest.astype(BF16)
    return hi, mid, (rest - mid.astype(F32)).astype(BF16)


def load_windows(ref, height, breadth):
    parts = []
    for r in range(0, height, WIN):
        for c in range(0, breadth, WIN):
            piece = ref[r : r + WIN, c : c + WIN, :].astype(F32)
            parts.append(piece.reshape(WIN * WIN, piece.shape[-1]))
    return jnp.concatenate(parts, axis=0)


def store_windows(ref, values, height, breadth):
    at = 0
    for r in range(0, height, WIN):
        for c in range(0, breadth, WIN):
            piece = values[at : at + WIN * WIN].reshape(WIN, WIN, values.shape[-1])
            ref[r : r + WIN, c : c + WIN, :] = piece.astype(ref.dtype)
            at += WIN * WIN


def edges(shape, direction):
    half = WIN // 2
    leave, land = [], []
    for size in shape[:2]:
        first, rest = slice(0, half), slice(half, size)
        body, last = slice(0, size - half), slice(size - half, size)
        leave.append((rest, first) if direction < 0 else (body, last))
        land.append((body, last) if direction < 0 else (rest, first))
    order = ((0, 0), (1, 0), (0, 1), (1, 1))
    return (
        [(leave[0][a], leave[1][b]) for a, b in order],
        [(land[0][a], land[1][b]) for a, b in order],
    )


def strip_shapes(shape):
    half = WIN // 2
    height, breadth, channels = shape
    return [(half, breadth - half, channels), (height - half, half, channels), (half, half, channels)]


def store_strips(refs, tile, direction):
    for ref, at in zip(refs, edges(tile.shape, direction)[0][1:]):
        ref[...] = tile[at].astype(ref.dtype)


def join_tile(scratch, tile_ref, strip_refs, direction):
    leave, land = edges(tile_ref.shape, direction)
    scratch[land[0]] = tile_ref[...].astype(F32)[leave[0]]
    for ref, at in zip(strip_refs, land[1:]):
        scratch[at] = ref[...].astype(F32)


def norm_parts(x):
    center = x - jnp.mean(x, axis=-1, keepdims=True)
    spread = jnp.mean(center * center, axis=-1, keepdims=True)
    inv = lax.rsqrt(spread + EPSILON)
    return center * inv, inv


def norm_back(unit, inv, gain, grad):
    scaled = grad * gain
    m1 = jnp.mean(scaled, axis=-1, keepdims=True)
    m2 = jnp.mean(scaled * unit, axis=-1, keepdims=True)
    return inv * (scaled - m1 - unit * m2)


def rnd(x):
    return x.astype(BF16).astype(F32)


def head_rows(rows, heads, size):
    lane = lax.broadcasted_iota(jnp.int32, (heads * rows, heads * size), 1)
    row = lax.broadcasted_iota(jnp.int32, (heads * rows, heads * size), 0)
    return (lane // size) == (row // rows)


def spread_heads(x, mask, heads):
    tiled = jnp.concatenate([x] * heads, axis=0)
    return jnp.where(mask, tiled, jnp.zeros_like(tiled))


def fold_heads(x, mask, heads, rows):
    kept = jnp.where(mask, x, 0.0)
    total = kept[:rows]
    for h in range(1, heads):
        total = total + kept[h * rows : (h + 1) * rows]
    return total


def cell_code(n, dim, shape):
    index = lax.broadcasted_iota(jnp.int32, shape, dim)
    return (index // WIN) * (2 * WIN - 1) + index % WIN


def position_stack(rel, heads):
    cells = WIN * WIN
    span = 2 * WIN - 1
    middle = (span * span - 1) // 2
    width = 256
    lanes = lax.broadcasted_iota(jnp.int32, (cells, 128), 1)
    pick = (lanes == cell_code(cells, 0, (cells, 128))).astype(BF16)
    outs = []
    for h in range(heads):
        row = jnp.concatenate([rel[h], jnp.zeros((1, width - span * span), F32)], axis=1)
        row = jnp.broadcast_to(row, (WIN, width))
        rolled = [
            pltpu.roll(row, (span * y - middle) % width, 1, stride=1, stride_axis=0)[:, :128]
            for y in range(WIN)
        ]
        parts = split3(jnp.concatenate(rolled, axis=0))
        outs.append(mm_nt(pick, parts[0]) + mm_nt(pick, parts[1]) + mm_nt(pick, parts[2]))
    return jnp.concatenate(outs, axis=0)


def position_grad(dstack, heads):
    cells = WIN * WIN
    span = 2 * WIN - 1
    middle = (span * span - 1) // 2
    width = 256
    lanes = lax.broadcasted_iota(jnp.int32, (cells, width), 1)
    pick = (lanes == middle - cell_code(cells, 0, (cells, width))).astype(BF16)
    rows = []
    for h in range(heads):
        hi, mid, _ = split3(dstack[h * cells : (h + 1) * cells])
        flipped = mm_tn(hi, pick) + mm_tn(mid, pick)
        total = None
        for y in range(WIN):
            part = pltpu.roll(
                flipped[y * WIN : (y + 1) * WIN], span * y, 1, stride=1, stride_axis=0
            )
            total = part if total is None else total + part
        rows.append(jnp.sum(total, axis=0, keepdims=True))
    rows.append(jnp.zeros((16 - heads, width), F32))
    stacked = jnp.concatenate(rows, axis=0)
    back = (
        lax.broadcasted_iota(jnp.int32, (width, width), 0)
        + lax.broadcasted_iota(jnp.int32, (width, width), 1)
        == span * span - 1
    ).astype(BF16)
    hi, mid, _ = split3(stacked)
    return mm(hi, back) + mm(mid, back)


def zone_masks(start_ref, height, breadth, total_rows, total_cols, heads):
    cells = WIN * WIN
    masks = []
    for r in range(0, height, WIN):
        for c in range(0, breadth, WIN):

            def zone(dim):
                index = lax.broadcasted_iota(jnp.int32, (heads * cells, cells), dim) % cells
                row = start_ref[0] + r + index // WIN
                col = start_ref[1] + c + index % WIN
                zr = (row >= total_rows - WIN).astype(jnp.int32) + (
                    row >= total_rows - WIN // 2
                ).astype(jnp.int32)
                zc = (col >= total_cols - WIN).astype(jnp.int32) + (
                    col >= total_cols - WIN // 2
                ).astype(jnp.int32)
                return zr * 3 + zc

            masks.append(zone(0) == zone(1))
    return masks


def attend(q_stack, k, position, mask, scale):
    scores = mm_nt(q_stack, k) * scale + position
    if mask is not None:
        scores = jnp.where(mask, scores, -1e30)
    powers = jnp.exp(scores - jnp.max(scores, axis=-1, keepdims=True))
    return powers / jnp.sum(powers, axis=-1, keepdims=True)


def forward(x, w, position, masks, heads):
    cells = WIN * WIN
    channels = x.shape[1]
    size = channels // heads
    unit, _ = norm_parts(x)
    normed = (unit * w["ng"][...] + w["nb"][...]).astype(BF16)
    packed = (mm(normed, w["wqkv"][0]) + w["bqkv"][...]).astype(BF16)
    hmask = head_rows(cells, heads, size)
    mixed = []
    for n in range(x.shape[0] // cells):
        at = slice(n * cells, (n + 1) * cells)
        q = packed[at, :channels]
        k = packed[at, channels : 2 * channels]
        v = packed[at, 2 * channels :]
        probs = attend(
            spread_heads(q, hmask, heads), k, position, None if masks is None else masks[n],
            size ** (-0.5),
        )
        mixed.append(fold_heads(mm(probs.astype(BF16), v), hmask, heads, cells).astype(BF16))
    mixed = jnp.concatenate(mixed, axis=0)
    mid = (x + mm(mixed, w["wproj"][0]) + w["bproj"][...]).astype(BF16)
    mid32 = mid.astype(F32)
    unit2, _ = norm_parts(mid32)
    normed2 = (unit2 * w["mg"][...] + w["mb"][...]).astype(BF16)
    pre = mm(normed2, w["wup"][0]) + w["bup"][...]
    half = 0.5 * (1.0 + lax.erf(pre * (2.0**-0.5)))
    hidden = (pre * half).astype(BF16)
    out = (mid32 + mm_nt(hidden, w["wdown"][0]) + w["bdown"][...]).astype(BF16)
    return out, (packed, mixed, mid, pre)


def backward(x, g, saved, w, position, masks, heads, grads_ref, light_ref):
    packed, mixed, mid, pre = saved
    cells = WIN * WIN
    channels = x.shape[1]
    size = channels // heads
    scale = size ** (-0.5)
    light_ref[...] = jnp.zeros_like(light_ref)
    g16 = g.astype(BF16)
    half = 0.5 * (1.0 + lax.erf(pre * (2.0**-0.5)))
    slope = half + pre * jnp.exp(-0.5 * pre * pre) * 0.3989422804014327
    hidden = (pre * half).astype(BF16)
    grads_ref[2 * channels : 3 * channels, :] = mm_tn(g16, hidden).astype(BF16)
    light_ref[3:4, :channels] = jnp.sum(g, axis=0, keepdims=True)
    dpre = rnd(mm(g16, w["wdown"][0])) * slope
    light_ref[0:1, : dpre.shape[1]] = jnp.sum(dpre, axis=0, keepdims=True)
    dpre16 = dpre.astype(BF16)
    mid32 = mid.astype(F32)
    unit2, inv2 = norm_parts(mid32)
    normed2 = (unit2 * w["mg"][...] + w["mb"][...]).astype(BF16)
    grads_ref[channels : 2 * channels, :] = mm_tn(normed2, dpre16).astype(BF16)
    dn2 = rnd(mm_nt(dpre16, w["wup"][0]))
    light_ref[2:3, 2 * channels : 3 * channels] = jnp.sum(dn2 * unit2, axis=0, keepdims=True)
    light_ref[2:3, 3 * channels : 4 * channels] = jnp.sum(dn2, axis=0, keepdims=True)
    dmid = rnd(rnd(norm_back(unit2, inv2, w["mg"][...], dn2)) + g)
    dmid16 = dmid.astype(BF16)
    light_ref[1:2, 3 * channels : 4 * channels] = jnp.sum(dmid, axis=0, keepdims=True)
    grads_ref[0:channels, 3 * channels : 4 * channels] = mm_tn(mixed, dmid16).astype(BF16)
    dmixed = mm_nt(dmid16, w["wproj"][0]).astype(BF16)
    hmask = head_rows(cells, heads, size)
    dpacked = []
    dposition = None
    for n in range(x.shape[0] // cells):
        at = slice(n * cells, (n + 1) * cells)
        q_stack = spread_heads(packed[at, :channels], hmask, heads)
        k = packed[at, channels : 2 * channels]
        v = packed[at, 2 * channels :]
        probs = attend(q_stack, k, position, None if masks is None else masks[n], scale)
        d_stack = spread_heads(dmixed[at], hmask, heads)
        dprobs = rnd(mm_nt(d_stack, v))
        dv = mm_tn(probs.astype(BF16), d_stack)
        ds = probs * (dprobs - jnp.sum(probs * dprobs, axis=-1, keepdims=True))
        dposition = ds if dposition is None else dposition + ds
        ds16 = (ds * scale).astype(BF16)
        dq = fold_heads(mm(ds16, k), hmask, heads, cells)
        dk = mm_tn(ds16, q_stack)
        dpacked.append(jnp.concatenate([dq, dk, dv], axis=1).astype(BF16))
    light_ref[4 : 4 + 12, 0:256] = position_grad(dposition, heads)[:12]
    dpacked = jnp.concatenate(dpacked, axis=0)
    light_ref[1:2, : 3 * channels] = jnp.sum(dpacked.astype(F32), axis=0, keepdims=True)
    unit, inv = norm_parts(x)
    normed = (unit * w["ng"][...] + w["nb"][...]).astype(BF16)
    grads_ref[0:channels, : 3 * channels] = mm_tn(normed, dpacked).astype(BF16)
    dn = rnd(mm_nt(dpacked, w["wqkv"][0]))
    light_ref[2:3, 0:channels] = jnp.sum(dn * unit, axis=0, keepdims=True)
    light_ref[2:3, channels : 2 * channels] = jnp.sum(dn, axis=0, keepdims=True)
    dx = rnd(norm_back(unit, inv, w["ng"][...], dn)) + dmid
    grads_ref[3 * channels : 3 * channels + 16, :] = light_ref[...].astype(BF16)
    rest = grads_ref.shape[0] - 3 * channels - 16
    if rest:
        grads_ref[3 * channels + 16 :, :] = jnp.zeros((rest, grads_ref.shape[1]), BF16)
    return dx


KEYS = ("ng", "nb", "wqkv", "bqkv", "rel", "wproj", "bproj", "mg", "mb", "wup", "bup", "wdown", "bdown")
MATRICES = ("wqkv", "wproj", "wup", "wdown")


def weight_view(refs, block):
    view = {}
    for key, ref in zip(KEYS, refs):
        if key == "rel":
            view[key] = [ref[h, block : block + 1, :] for h in range(ref.shape[0])]
        else:
            view[key] = ref if key in MATRICES else ref.at[block : block + 1, :]
    return view


def weight_specs(params, block):
    specs = []
    for key, member in zip(KEYS, params):
        if key in MATRICES:
            specs.append(pl.BlockSpec((1,) + member.shape[1:], lambda i: (block, 0, 0)))
        else:
            specs.append(whole(member.shape))
    return specs


def whole(shape):
    return pl.BlockSpec(shape, lambda i: (0,) * len(shape))


def shape_of(shape, dtype):
    return jax.ShapeDtypeStruct(shape, dtype)


def first_forward(imagery, params):
    height, breadth, channels = imagery.shape
    heads = params[4].shape[0]
    tokens = height * breadth
    mlp = params[9].shape[2]

    def body(x_ref, *refs):
        w = weight_view(refs[: len(KEYS)], 0)
        out_ref, packed_ref, mixed_ref, mid_ref, pre_ref, pos_ref = refs[len(KEYS) : len(KEYS) + 6]
        strip_refs, tile = refs[len(KEYS) + 6 : len(KEYS) + 9], refs[-1]
        x = load_windows(x_ref, height, breadth)
        position = position_stack(w["rel"], heads)
        pos_ref[...] = position
        out, saved = forward(x, w, position, None, heads)
        store_windows(tile, out.astype(F32), height, breadth)
        moved = tile[...]
        out_ref[...] = moved.astype(BF16)
        store_strips(strip_refs, moved, -1)
        for ref, value in zip((packed_ref, mixed_ref, mid_ref, pre_ref), saved):
            ref[...] = value

    outs = [
        shape_of(imagery.shape, BF16),
        shape_of((tokens, 3 * channels), BF16),
        shape_of((tokens, channels), BF16),
        shape_of((tokens, channels), BF16),
        shape_of((tokens, mlp), F32),
        shape_of((heads * WIN * WIN, WIN * WIN), F32),
    ] + [shape_of(strip, BF16) for strip in strip_shapes(imagery.shape)]
    return pl.pallas_call(
        body,
        name="fwd0",
        grid=(1,),
        out_shape=outs,
        in_specs=[whole(imagery.shape)] + weight_specs(params, 0),
        out_specs=[whole(o.shape) for o in outs],
        scratch_shapes=[pltpu.VMEM(imagery.shape, F32)],
    )(imagery, *params)


def second_both(moved, moved_strips, grad, grad_strips, start, params, total_rows, total_cols, grad_rows):
    height, breadth, channels = moved.shape
    heads = params[4].shape[0]
    width = params[9].shape[2]

    def body(start_ref, x_ref, g_ref, *refs):
        tile, light_ref = refs[-2:]
        join_tile(tile, x_ref, refs[:3], -1)
        x = load_windows(tile, height, breadth)
        join_tile(tile, g_ref, refs[3:6], -1)
        g = load_windows(tile, height, breadth)
        refs = refs[6:]
        w = weight_view(refs[: len(KEYS)], 1)
        out_ref, dx_ref, grads_ref = refs[len(KEYS) : len(KEYS) + 3]
        out_strips, dx_strips = refs[len(KEYS) + 3 : len(KEYS) + 6], refs[len(KEYS) + 6 : len(KEYS) + 9]
        position = position_stack(w["rel"], heads)
        masks = zone_masks(start_ref, height, breadth, total_rows, total_cols, heads)
        out, saved = forward(x, w, position, masks, heads)
        dx = backward(x, g, saved, w, position, masks, heads, grads_ref, light_ref)
        for ref, strips, value in (
            (out_ref, out_strips, out.astype(F32)),
            (dx_ref, dx_strips, dx),
        ):
            store_windows(tile, value, height, breadth)
            whole_tile = tile[...]
            ref[...] = whole_tile.astype(BF16)
            store_strips(strips, whole_tile, 1)

    outs = [
        shape_of(moved.shape, BF16),
        shape_of(moved.shape, BF16),
        shape_of((grad_rows, width), BF16),
    ] + [shape_of(strip, BF16) for strip in strip_shapes(moved.shape) * 2]
    return pl.pallas_call(
        body,
        name="both1",
        grid=(1,),
        out_shape=outs,
        in_specs=[pl.BlockSpec(memory_space=pltpu.SMEM), whole(moved.shape), whole(moved.shape)]
        + [whole(strip.shape) for strip in (*moved_strips, *grad_strips)]
        + weight_specs(params, 1),
        out_specs=[whole(o.shape) for o in outs],
        scratch_shapes=[pltpu.VMEM(moved.shape, F32), pltpu.VMEM((16, width), F32)],
    )(start, moved, grad, *moved_strips, *grad_strips, *params)


def first_backward(imagery, grad, grad_strips, saved, params, grad_rows):
    height, breadth, channels = imagery.shape
    heads = params[4].shape[0]
    width = params[9].shape[2]

    def body(x_ref, g_ref, packed_ref, mixed_ref, mid_ref, pre_ref, pos_ref, *refs):
        w = weight_view(refs[: len(KEYS)], 0)
        strip_refs = refs[len(KEYS) : len(KEYS) + 3]
        dx_ref, grads_ref, tile, light_ref = refs[len(KEYS) + 3 :]
        x = load_windows(x_ref, height, breadth)
        join_tile(tile, g_ref, strip_refs, 1)
        g = load_windows(tile, height, breadth)
        values = (packed_ref[...], mixed_ref[...], mid_ref[...], pre_ref[...])
        dx = backward(x, g, values, w, pos_ref[...], None, heads, grads_ref, light_ref)
        store_windows(dx_ref, dx, height, breadth)

    outs = [shape_of(imagery.shape, BF16), shape_of((grad_rows, width), BF16)]
    return pl.pallas_call(
        body,
        name="bwd0",
        grid=(1,),
        out_shape=outs,
        in_specs=[whole(imagery.shape), whole(grad.shape)]
        + [whole(s.shape) for s in saved]
        + weight_specs(params, 0)
        + [whole(strip.shape) for strip in grad_strips],
        out_specs=[whole(o.shape) for o in outs],
        scratch_shapes=[pltpu.VMEM(imagery.shape, F32), pltpu.VMEM((16, width), F32)],
    )(imagery, grad, *saved, *params, *grad_strips)


def sum_all(grads_one, grads_two, nz, nq):
    block_rows, width = grads_one.shape
    rows = 2 * block_rows
    half = width // 2
    unit = nq * nz * 16
    count = rows // unit
    part = unit // nq
    piece = 16
    per_chunk = 2 * nq + 2 * nz - 1

    def body(one_ref, two_ref, out_ref, buf0, acc, buf1, acc1, buf2, send, recv):
        z = lax.axis_index("rows")
        col = lax.axis_index("cols")
        core = lax.rem(col, 2)
        q = col // 2
        mine = pl.multiple_of(core * half, 128)
        other = pl.multiple_of((1 - core) * half, 128)
        partner = (z, q * 2 + (1 - core))
        across = [(z, lax.rem(q + d, nq) * 2 + core) for d in range(1, nq)]
        along = [(lax.rem(z + d, nz), col) for d in range(1, nz)]
        barrier = pltpu.get_barrier_semaphore()
        for peer in [partner] + across + along:
            pl.semaphore_signal(barrier, inc=1, device_id=peer, device_id_type=MESH)
        pl.semaphore_wait(barrier, nq + nz - 1)
        lanes = pl.ds(mine, half)
        pending = {}

        def copy(chunk, slot, src, dst, peer):
            index = chunk * per_chunk + slot
            c = pltpu.make_async_remote_copy(
                src_ref=src,
                dst_ref=dst,
                send_sem=send.at[index],
                recv_sem=recv.at[index],
                device_id=peer,
                device_id_type=MESH,
            )
            c.start()
            pending.setdefault(chunk, []).append(c)

        def finish(chunk):
            for c in pending.pop(chunk):
                c.wait()

        def pieces(chunk):
            low, high = chunk * unit, (chunk + 1) * unit
            found = []
            for b, ref in ((1, two_ref), (0, one_ref)):
                base = (1 - b) * block_rows
                lo, hi = max(low, base), min(high, base + block_rows)
                if lo < hi:
                    found.append((ref, lo - base, lo - low, hi - lo))
            return found

        def stage0(c):
            for place, (ref, at, to, size) in enumerate(pieces(c)):
                copy(
                    c,
                    place,
                    ref.at[at : at + size, pl.ds(other, half)],
                    buf0.at[c * unit + to : c * unit + to + size, :],
                    partner,
                )

        def stage1(c):
            finish(c)
            for ref, at, to, size in pieces(c):
                where = slice(c * unit + to, c * unit + to + size)
                acc[where, :] = (
                    ref[at : at + size, lanes].astype(F32) + buf0[where, :].astype(F32)
                ).astype(BF16)
            for d in range(1, nq):
                to = pl.multiple_of(c * unit + lax.rem(q + d, nq) * part, 16)
                copy(c, 1 + d, acc.at[pl.ds(to, part), :], buf1.at[c, d - 1], across[d - 1])

        def stage2(c):
            finish(c)
            total = acc[pl.ds(pl.multiple_of(c * unit + q * part, 16), part), :].astype(F32)
            for d in range(1, nq):
                total = total + buf1[c, d - 1].astype(F32)
            acc1[c] = total.astype(BF16)
            for d in range(1, nz):
                to = pl.multiple_of(lax.rem(z + d, nz) * piece, 16)
                copy(c, nq + d, acc1.at[c, pl.ds(to, piece), :], buf2.at[c, d - 1], along[d - 1])

        def stage3(c):
            finish(c)
            total = acc1[c, pl.ds(pl.multiple_of(z * piece, 16), piece), :].astype(F32)
            for d in range(1, nz):
                total = total + buf2[c, d - 1].astype(F32)
            own = pl.ds(pl.multiple_of(c * unit + q * part + z * piece, 16), piece)
            out_ref[own, lanes] = total.astype(BF16)
            for d in range(1, nz):
                copy(c, nq + nz - 1 + d, out_ref.at[own, lanes], out_ref.at[own, lanes], along[d - 1])

        def stage4(c):
            finish(c)
            own = pl.ds(pl.multiple_of(c * unit + q * part, 16), part)
            for d in range(1, nq):
                copy(c, nq + 2 * nz - 2 + d, out_ref.at[own, lanes], out_ref.at[own, lanes], across[d - 1])

        def stage5(c):
            finish(c)
            own = slice(c * unit, (c + 1) * unit)
            copy(c, 2 * nq + 2 * nz - 2, out_ref.at[own, lanes], out_ref.at[own, lanes], partner)

        stages = (stage1, stage2, stage3, stage4, stage5, finish)
        for c in range(count):
            stage0(c)
        for tick in range(count + len(stages) - 1):
            for c in range(count):
                if 0 <= tick - c < len(stages):
                    stages[tick - c](c)

    sems = per_chunk * count
    vmem = pl.BlockSpec(memory_space=pltpu.VMEM)
    return pl.pallas_call(
        body,
        name="sum_all",
        out_shape=shape_of((rows, width), BF16),
        in_specs=[vmem, vmem],
        out_specs=vmem,
        scratch_shapes=[
            pltpu.VMEM((rows, half), BF16),
            pltpu.VMEM((rows, half), BF16),
            pltpu.VMEM((count, max(nq - 1, 1), part, half), BF16),
            pltpu.VMEM((count, part, half), BF16),
            pltpu.VMEM((count, max(nz - 1, 1), piece, half), BF16),
            pltpu.SemaphoreType.DMA((sems,)),
            pltpu.SemaphoreType.DMA((sems,)),
        ],
        compiler_params=pltpu.CompilerParams(collective_id=0, has_side_effects=True),
    )(grads_one, grads_two)


def unpack(summed, params, factor):
    channels = params[0].shape[1]
    heads, _, offsets = params[4].shape
    block_rows = summed.shape[0] // 2

    def body(s_ref, *outs):
        o = dict(zip(KEYS, outs))
        for b in range(2):
            at = (1 - b) * block_rows

            def rows(low, count):
                return s_ref[at + low : at + low + count, :].astype(F32) * factor

            top = rows(0, channels)
            o["wqkv"][b] = top[:, : 3 * channels]
            o["wproj"][b] = top[:, 3 * channels :]
            o["wup"][b] = rows(channels, channels)
            o["wdown"][b] = rows(2 * channels, channels)
            light = rows(3 * channels, 16)
            o["bup"][b : b + 1, :] = light[0:1, :]
            o["bqkv"][b : b + 1, :] = light[1:2, : 3 * channels]
            o["bproj"][b : b + 1, :] = light[1:2, 3 * channels :]
            for place, key in enumerate(("ng", "nb", "mg", "mb")):
                o[key][b : b + 1, :] = light[2:3, place * channels : (place + 1) * channels]
            o["bdown"][b : b + 1, :] = light[3:4, :channels]
            for h in range(heads):
                o["rel"][h, b : b + 1, :] = light[4 + h : 5 + h, :offsets]

    outs = [shape_of(member.shape, F32) for member in params]
    return pl.pallas_call(
        body,
        name="unpack",
        grid=(1,),
        out_shape=outs,
        in_specs=[whole(summed.shape)],
        out_specs=[whole(o.shape) for o in outs],
    )(summed)


def travel(strips, direction):
    nz, nc = lax.axis_size("rows"), lax.axis_size("cols")
    rows = [(i, (i + direction) % nz) for i in range(nz)]
    cols = [(i, (i + direction) % nc) for i in range(nc)]
    both = [
        (r * nc + c, (r + direction) % nz * nc + (c + direction) % nc)
        for r in range(nz)
        for c in range(nc)
    ]
    return [
        lax.ppermute(strips[0], "rows", rows),
        lax.ppermute(strips[1], "cols", cols),
        lax.ppermute(strips[2], ("rows", "cols"), both),
    ]


def per_device(imagery, cotangent, *params):
    height, breadth, channels = imagery.shape
    nz = lax.axis_size("rows")
    nc = lax.axis_size("cols")
    total_rows = height * nz
    total_cols = breadth * nc
    params = list(params)
    params[4] = jnp.swapaxes(params[4], 0, 1)
    params[11] = jnp.swapaxes(params[11], 1, 2)
    start = jnp.stack(
        [lax.axis_index("rows") * height, lax.axis_index("cols") * breadth]
    ).astype(jnp.int32)
    unit = nz * (nc // 2) * 8
    grad_rows = -(-(3 * channels + 16) // unit) * unit
    grad_strips = travel([cotangent[at] for at in edges(cotangent.shape, -1)[0][1:]], -1)
    level_one, *rest = first_forward(imagery, params)
    saved, strips = rest[:5], rest[5:]
    level_two, back_two, grads_two, *strips = second_both(
        level_one,
        travel(strips, -1),
        cotangent,
        grad_strips,
        start,
        params,
        total_rows,
        total_cols,
        grad_rows,
    )
    back_strips = travel(strips[3:], 1)
    back_one, grads_one = first_backward(imagery, back_two, back_strips, saved, params, grad_rows)
    half = WIN // 2
    row_strip, col_strip, corner = travel(strips[:3], 1)
    output = jnp.concatenate(
        [
            jnp.concatenate([corner, row_strip], axis=1),
            jnp.concatenate([col_strip, level_two[:-half, :-half]], axis=1),
        ],
        axis=0,
    )
    summed = sum_all(grads_one, grads_two, nz, nc // 2)
    merged = unpack(summed, params, float(total_rows * total_cols) ** (-0.5))
    merged = list(merged)
    merged[4] = jnp.swapaxes(merged[4], 0, 1)
    merged[11] = jnp.swapaxes(merged[11], 1, 2)
    return (output, back_one) + tuple(merged)


def solution(mesh):
    tile = P("rows", "cols", None)
    return jax.shard_map(
        per_device,
        mesh=mesh,
        in_specs=(tile, tile) + (P(),) * 13,
        out_specs=(tile, tile) + (P(),) * 13,
        check_vma=False,
    )
```
